32 devices in a mesh: rep: 4 (over y, core), shard: 8 (over z, x).
Axes of the slice: x: 2, y: 2, z: 4, core: 2. Of those that a mesh axis runs over, the one named last changes fastest.
Arguments:
- image: bfloat16 [32, 1024, 1024], P(('rep', 'shard')), may hold values from -6 to 6
- timestep: int32 [32], P(('rep', 'shard')), may hold values from 0 to 999
- label: int32 [32], P(('rep', 'shard')), may hold values from 0 to 1000
- label_table: bfloat16 [1001, 1024], P(None, 'shard'), may hold values from -6 to 6
- ada_weight: bfloat16 [1024, 6144], P('shard'), may hold values from -0.1875 to 0.1875
- ada_bias: bfloat16 [6144], P('shard'), may hold values from -3 to 3
- qkv_weight: bfloat16 [1024, 3072], P('shard'), may hold values from -0.1875 to 0.1875
- qv_bias: bfloat16 [2048], P('shard'), may hold values from -3 to 3
- out_weight: bfloat16 [1024, 1024], P('shard'), may hold values from -0.75 to 0.75
- out_bias: bfloat16 [1024], P('shard'), may hold values from -3 to 3
- up_weight: bfloat16 [1024, 4096], P('shard'), may hold values from -0.1875 to 0.1875
- up_bias: bfloat16 [4096], P('shard'), may hold values from -3 to 3
- down_weight: bfloat16 [4096, 1024], P('shard'), may hold values from -0.09375 to 0.09375
- down_bias: bfloat16 [1024], P('shard'), may hold values from -3 to 3
- grad_out: bfloat16 [32, 1024, 1024], P(('rep', 'shard')), may hold values from -6 to 6
Outputs:
- output: bfloat16 [32, 1024, 1024], P(('rep', 'shard'))
- grad_image: float32 [32, 1024, 1024], P(('rep', 'shard'))
- grad_cond: float32 [32, 1024], P(('rep', 'shard'))
- grad_table: float32 [1001, 1024], P(None, 'shard')
- grad_ada_weight: float32 [1024, 6144], P('shard')
- grad_ada_bias: float32 [6144], P('shard')
- grad_qkv_weight: float32 [1024, 3072], P('shard')
- grad_qv_bias: float32 [2048], P('shard')
- grad_out_weight: float32 [1024, 1024], P('shard')
- grad_out_bias: float32 [1024], P('shard')
- grad_up_weight: float32 [1024, 4096], P('shard')
- grad_up_bias: float32 [4096], P('shard')
- grad_down_weight: float32 [4096, 1024], P('shard')
- grad_down_bias: float32 [1024], P('shard')
The draws below stay inside these ranges and needn't reach their ends.
All inputs are finite; a program needn't handle non-finite values.
Results may differ from the reference program's by a relative error of at most 0.017.
The reference program's roundings to bfloat16 on the way count: a program that leaves them out, or rounds other values in their place, can miss the bound.
Values may be sent and summed in bfloat16 or wider, within the bound.
No kernel may reach another device: no remote copies, remote signals or barrier semaphores. Data moves between devices by JAX's collectives and lax.ppermute only.
A program may use at most 256 MiB of HBM per device.

```python
import math
import jax
import jax.numpy as jnp
from jax import lax

D = 1024
HEADS = 16
HEAD = 64
MLP = 4096
CLASSES = 1001
LEN = 1024
IMAGES = 32


def place_ends(drawn, key, low, high):
    spot = [jax.random.randint(jax.random.fold_in(key, axis), (), 0, length) for axis, length in enumerate(drawn.shape)]
    widest = drawn.shape.index(max(drawn.shape))
    beside = spot[:widest] + [(spot[widest] + 1) % drawn.shape[widest]] + spot[widest + 1:]
    return drawn.at[tuple(spot)].set(low).at[tuple(beside)].set(high)


def block_scale(own_key, dims, cuts, smallest, top_value):
    loudness = 1.0
    for position, parts in cuts:
        steps = jax.random.uniform(jax.random.fold_in(jax.random.fold_in(own_key, 6), position), (parts,), jnp.float32, smallest / len(cuts), top_value / len(cuts))
        loudness = loudness * jnp.repeat(jnp.exp(steps), dims[position] // parts).reshape((-1,) + (1,) * (len(dims) - 1 - position))
    return loudness


def normal_values(own_key, dims, deviation, most, cuts=(), kind=jnp.bfloat16):
    level = block_scale(own_key, dims, cuts, -0.22, 0.18) if cuts else 1.0
    drawn = jax.random.normal(own_key, dims, jnp.float32) * deviation * level
    return jnp.minimum(jnp.maximum(drawn, -most), most).astype(kind)


def setup_inputs(seed: int = 0) -> dict:
    keys = jax.random.split(jax.random.key(seed), 16)
    image = normal_values(keys[0], (IMAGES, LEN, D), 1.0, 6.0, ((0, 32),))
    timestep = place_ends(jax.random.randint(keys[1], (IMAGES,), 0, 1000), jax.random.fold_in(keys[1], 1), 0, 999).astype(jnp.int32)
    label = place_ends(jax.random.randint(keys[2], (IMAGES,), 0, CLASSES), jax.random.fold_in(keys[2], 1), 0, CLASSES - 1).astype(jnp.int32)
    label_table = normal_values(keys[3], (CLASSES, D), 1.0, 6.0, ((1, 8),))
    ada_weight = normal_values(keys[4], (D, 6 * D), D ** -0.5, 0.1875, ((0, 8),))
    ada_bias = normal_values(keys[5], (6 * D,), 0.5, 3.0, ((0, 8),))
    qkv_weight = normal_values(keys[6], (D, 3 * D), D ** -0.5, 0.1875, ((0, 8),))
    qv_bias = normal_values(keys[7], (2 * D,), 0.5, 3.0, ((0, 8),))
    out_weight = normal_values(keys[8], (D, D), (D // 16) ** -0.5, 0.75, ((0, 8),))
    out_bias = normal_values(keys[9], (D,), 0.5, 3.0, ((0, 8),))
    up_weight = normal_values(keys[10], (D, MLP), D ** -0.5, 0.1875, ((0, 8),))
    up_bias = normal_values(keys[11], (MLP,), 0.5, 3.0, ((0, 8),))
    down_weight = normal_values(keys[12], (MLP, D), MLP ** -0.5, 0.09375, ((0, 8),))
    down_bias = normal_values(keys[13], (D,), 0.5, 3.0, ((0, 8),))
    grad_out = normal_values(keys[14], (IMAGES, LEN, D), 1.0, 6.0, ((0, 32),))
    return dict(image=image, timestep=timestep, label=label, label_table=label_table, ada_weight=ada_weight, ada_bias=ada_bias, qkv_weight=qkv_weight, qv_bias=qv_bias, out_weight=out_weight, out_bias=out_bias, up_weight=up_weight, up_bias=up_bias, down_weight=down_weight, down_bias=down_bias, grad_out=grad_out)


@jax.custom_vjp
def low(v):
    return lax.optimization_barrier(v.astype(jnp.bfloat16)).astype(jnp.float32)

@jax.custom_vjp
def low_back(v):
    return v

def low_keep(v):
    return (low(v), None)

def low_pass(kept, grad):
    return (grad,)

def back_keep(v):
    return (v, None)

def back_low(kept, grad):
    return (low(grad),)
low.defvjp(low_keep, low_pass)
low_back.defvjp(back_keep, back_low)

def matmul(left, right):
    return jnp.dot(left, right, precision=lax.Precision.HIGHEST, preferred_element_type=jnp.float32)

def layer_norm(values):
    center = values - lax.optimization_barrier(jnp.mean(values, axis=-1, keepdims=True))
    spread = lax.optimization_barrier(jnp.mean(center * center, axis=-1, keepdims=True))
    return center * lax.rsqrt(spread + 1e-06)

def timestep_features(timestep, total_width):
    half_width = total_width // 2
    frequency = jnp.exp(-math.log(10000.0) * jnp.arange(half_width, dtype=jnp.float32) / half_width)
    angles = timestep.astype(jnp.float32)[:, None] * frequency[None, :]
    return jnp.concatenate([jnp.cos(angles), jnp.sin(angles)], axis=-1)

def head_attend(pieces):
    query_matrix_rows, key_matrix_rows, value_matrix_rows = pieces
    scores = low_back(matmul(query_matrix_rows, key_matrix_rows.T) * 0.125)
    attention_result = low(jax.nn.softmax(scores, axis=-1))
    return matmul(attention_result, value_matrix_rows)

def block_forward(params, picture, condition):
    ada_weight, ada_bias, qkv_weight, qv_bias, out_weight, out_bias, up_weight, up_bias, down_weight, down_bias = params
    silu_cond = low(jax.nn.silu(condition))
    modulation = low_back(matmul(silu_cond[None, :], ada_weight)[0] + ada_bias)
    shift_attn, scale_attn, attention_gate, shift_mlp, scale_mlp, gate_mlp = jnp.split(modulation, 6)
    normed = layer_norm(picture)
    hidden = low(normed * (1.0 + scale_attn) + shift_attn)
    full_bias = jnp.concatenate([qv_bias[:D], jnp.zeros_like(qv_bias[:D]), qv_bias[D:]])
    projected = low(low_back(matmul(hidden, qkv_weight) + full_bias))
    heads_all = projected.reshape(LEN, 3, HEADS, HEAD).transpose(1, 2, 0, 3)
    mixed_heads = lax.map(jax.checkpoint(head_attend), (heads_all[0], heads_all[1], heads_all[2]))
    merged = low(low_back(mixed_heads.transpose(1, 0, 2).reshape(LEN, D)))
    branch = low_back(matmul(merged, out_weight) + out_bias)
    middle = picture + attention_gate * branch
    normed_two = layer_norm(middle)
    hidden_two = low(normed_two * (1.0 + scale_mlp) + shift_mlp)
    inner_pre = low_back(matmul(hidden_two, up_weight) + up_bias)
    activated = low(jax.nn.gelu(inner_pre, approximate=True))
    second = low_back(matmul(activated, down_weight) + down_bias)
    return middle + gate_mlp * second

def reference(image, timestep, label, label_table, ada_weight, ada_bias, qkv_weight, qv_bias, out_weight, out_bias, up_weight, up_bias, down_weight, down_bias, grad_out):
    params = (ada_weight.astype(jnp.float32), ada_bias.astype(jnp.float32), qkv_weight.astype(jnp.float32), qv_bias.astype(jnp.float32), out_weight.astype(jnp.float32), out_bias.astype(jnp.float32), up_weight.astype(jnp.float32), up_bias.astype(jnp.float32), down_weight.astype(jnp.float32), down_bias.astype(jnp.float32))

    def make_condition(table_rows):
        return table_rows[label] + timestep_features(timestep, D)
    condition, condition_back = jax.vjp(make_condition, label_table.astype(jnp.float32))

    def per_image(totals, scan_items):
        picture, cond_row, cotangent = scan_items
        result, pullback = jax.vjp(block_forward, params, picture.astype(jnp.float32), cond_row)
        grad_params, grad_picture, grad_row = pullback(cotangent.astype(jnp.float32))
        totals = jax.tree.map(jnp.add, totals, grad_params)
        return (totals, (result.astype(jnp.bfloat16), grad_picture, grad_row))
    zero_grads = jax.tree.map(jnp.zeros_like, params)
    totals, stacked = lax.scan(per_image, zero_grads, (image, condition, grad_out))
    output, grad_image, grad_cond = stacked
    grad_table, = condition_back(grad_cond)
    return (output, grad_image, grad_cond, grad_table, totals[0], totals[1], totals[2], totals[3], totals[4], totals[5], totals[6], totals[7], totals[8], totals[9])
```

```python
import math

import jax
import jax.numpy as jnp
from jax import lax
from jax.experimental import pallas as pl
from jax.experimental.pallas import tpu as pltpu
from jax.sharding import PartitionSpec as P

HEADS = 16
HEAD = 64
PAIR = 2 * HEAD
EPS = 1e-06
LOG2E = math.log2(math.e)
SCALE2 = 0.125 * LOG2E
GELU_C = math.sqrt(2.0 / math.pi)

f32 = jnp.float32
bf16 = jnp.bfloat16

NN = (((1,), (0,)), ((), ()))
NT = (((1,), (1,)), ((), ()))
TN = (((0,), (0,)), ((), ()))


def mm(left, right, dims):
    return lax.dot_general(left, right, dims, preferred_element_type=f32)


def swap(values, axis, bits):
    size = lax.axis_size(axis)
    return lax.ppermute(values, axis, [(i, i ^ bits) for i in range(size)])


def bits_of(size):
    return [1 << b for b in range(size.bit_length() - 1)]


def gather_xor(values, axis, order):
    for bit in order:
        values = jnp.concatenate([values, swap(values, axis, bit)], axis=0)
    return values


def unxor(values, index, size):
    for bit in bits_of(size):
        shape = values.shape
        halves = values.reshape(size // (2 * bit), 2, bit, *shape[1:])
        flipped = jnp.concatenate([halves[:, 1:], halves[:, :1]], axis=1)
        values = jnp.where((index & bit) != 0, flipped, halves).reshape(shape)
    return values


def inner_size(shards):
    return 1 << ((shards.bit_length() - 1) // 2)


def gather_plane(piece, shards):
    inner = inner_size(shards)
    outer = shards // inner
    rows = [piece] + [swap(piece, "shard", k * inner) for k in range(1, outer)]
    stack = jnp.stack(rows)
    return [stack] + [swap(stack, "shard", j) for j in range(1, inner)]


def gather_full(parts, rep, shards):
    own = lax.dynamic_index_in_dim(parts, rep, 0, keepdims=True)
    zero = gather_plane(own, shards)
    two = [swap(buffer, "rep", 2) for buffer in zero]
    one = [swap(buffer, "rep", 1) for buffer in zero]
    three = [swap(buffer, "rep", 1) for buffer in two]
    return [(zero, 0), (one, 0), (two, 0), (three, 0)]


def gather_half(parts, rep, shards):
    own = jnp.stack(
        [lax.dynamic_index_in_dim(parts, rep ^ flip, 0, keepdims=False) for flip in (0, 2)]
    )
    zero = gather_plane(own, shards)
    one = [swap(buffer, "rep", 1) for buffer in zero]
    return [(zero, 0), (one, 0), (zero, 1), (one, 1)]


def scatter_sum(keep, send, shards):
    inner = inner_size(shards)
    outer = shards // inner
    from_core = swap(send, "rep", 1)

    def add(*terms):
        total = terms[0].astype(f32)
        for term in terms[1:]:
            total = total + term.astype(f32)
        return total

    from_y = swap(add(keep[0], from_core[0]).astype(bf16), "rep", 2)
    from_x = [
        swap(add(keep[1, j], from_core[1, j], from_y[j]).astype(bf16), "shard", j)
        for j in range(1, inner)
    ]

    def local(k):
        return add(
            keep[1, 0, k], from_core[1, 0, k], from_y[0, k], *[piece[k] for piece in from_x]
        )

    from_z = [swap(local(k).astype(bf16), "shard", k * inner) for k in range(1, outer)]
    return add(local(0), *from_z).astype(bf16)


def gather_quarters(own, rep):
    pair = jnp.stack([own, swap(own, "rep", 2)])
    pair = jnp.where((rep & 2) != 0, pair[::-1], pair)
    other = swap(pair, "rep", 1)
    both = jnp.stack([pair, other], axis=1)
    both = jnp.where((rep & 1) != 0, both[:, ::-1], both)
    return both.reshape(4, *own.shape)


def slice_copies(ids, source, target, sems, first):
    refs, t, columns = source
    inner = len(refs)
    outer = refs[0].shape[0]
    rows = refs[0].shape[2]
    copies = []
    for j, ref in enumerate(refs):
        for k in range(outer):
            at = pl.multiple_of((ids[1] ^ (k * inner + j)) * rows, rows)
            copies.append(
                pltpu.make_async_copy(
                    ref.at[k, t, :, columns],
                    target(pl.ds(at, rows)),
                    sems.at[first + len(copies)],
                )
            )
    return copies


def any_spec():
    return pl.BlockSpec(memory_space=pl.ANY)


def smem_spec():
    return pl.BlockSpec(memory_space=pltpu.SMEM)


def whole_spec(shape):
    return pl.BlockSpec(shape, lambda *g: (0,) * len(shape))


def flat_pieces(pieces):
    buffers, where = [], []
    for refs, t in pieces:
        spots = []
        for ref in refs:
            for n, known in enumerate(buffers):
                if known is ref:
                    spots.append(n)
                    break
            else:
                spots.append(len(buffers))
                buffers.append(ref)
        where.append((spots, t))
    return buffers, where


def params(limit=58):
    return pltpu.CompilerParams(vmem_limit_bytes=limit << 20)


def cost(flops, nbytes):
    return pl.CostEstimate(flops=int(flops), bytes_accessed=int(nbytes), transcendentals=0)


def norm_of(values):
    center = values - jnp.mean(values, axis=-1, keepdims=True)
    spread = jnp.mean(center * center, axis=-1, keepdims=True)
    inverse = lax.rsqrt(spread + EPS)
    return center * inverse, inverse


def norm_back(norm, inverse, grad):
    return inverse * (
        grad
        - jnp.mean(grad, axis=-1, keepdims=True)
        - norm * jnp.mean(grad * norm, axis=-1, keepdims=True)
    )


def qkv_forward(ids, image, mod, bias, pieces, tile=256):
    length, width = image.shape
    cols = 3 * width // 4
    buffers, where = flat_pieces(pieces)
    count = len(buffers)

    def kernel(ids_ref, image_ref, mod_ref, bias_ref, *rest):
        refs = rest[:count]
        h1_ref, out_ref, weight, sems = rest[count:]

        def copies(part):
            spots, t = where[part]
            source = ([refs[n] for n in spots], t, pl.ds(0, cols))
            size = len(spots) * refs[0].shape[0]
            return slice_copies(
                ids_ref, source, lambda rows: weight.at[part, rows, :], sems, part * size
            )

        first = pl.program_id(0) == 0

        @pl.when(first)
        def _():
            for part in range(4):
                for copy in copies(part):
                    copy.start()

        norm, _ = norm_of(image_ref[...].astype(f32))
        hidden = (norm * (1.0 + mod_ref[1:2, :]) + mod_ref[0:1, :]).astype(bf16)
        h1_ref[...] = hidden
        for part in range(4):

            @pl.when(first)
            def _():
                for copy in copies(part):
                    copy.wait()

            row = bias_ref[pl.ds(ids_ref[0] ^ part, 1), :]
            out_ref[:, part * cols : (part + 1) * cols] = (
                mm(hidden, weight[part], NN) + row
            ).astype(bf16)

    slots = 4 * len(where[0][0]) * buffers[0].shape[0]
    return pl.pallas_call(
        kernel,
        name="qkv_forward",
        grid=(length // tile,),
        in_specs=[
            smem_spec(),
            pl.BlockSpec((tile, width), lambda i: (i, 0)),
            whole_spec(mod.shape),
            whole_spec(bias.shape),
        ]
        + [any_spec()] * count,
        out_specs=[
            pl.BlockSpec((tile, width), lambda i: (i, 0)),
            pl.BlockSpec((tile, 3 * width), lambda i: (i, 0)),
        ],
        out_shape=[
            jax.ShapeDtypeStruct((length, width), bf16),
            jax.ShapeDtypeStruct((length, 3 * width), bf16),
        ],
        scratch_shapes=[
            pltpu.VMEM((4, width, cols), bf16),
            pltpu.SemaphoreType.DMA((slots,)),
        ],
        compiler_params=params(),
        cost_estimate=cost(6 * length * width * width, 18 * length * width),
    )(ids, image, mod, bias, *buffers)


def head_columns(width, kind):
    per_part = width // 4 // PAIR

    def index(p, ids):
        return 0, (p // per_part) * 3 * per_part + kind * per_part + p % per_part

    return index


def pair_columns(width):
    per_part = width // 4 // PAIR

    def index(p, ids):
        return 0, (ids[0] ^ (p // per_part)) * per_part + p % per_part

    return index


def attend_forward(ids, qkv, block=512):
    length, width3 = qkv.shape
    width = width3 // 3
    pairs = width // PAIR

    def kernel(ids_ref, q_ref, k_ref, v_ref, out_ref, lse_ref):
        left = lax.broadcasted_iota(jnp.int32, (1, PAIR), 1) < HEAD
        for b in range(length // block):
            rows = slice(b * block, (b + 1) * block)
            query = q_ref[rows, :]
            blank = jnp.zeros_like(query)
            mixed, logs = [], []
            for h in range(2):
                one = jnp.where(left, query, blank) if h == 0 else jnp.where(left, blank, query)
                scores = mm(one, k_ref[...], NT)
                peak = jnp.max(scores, axis=-1, keepdims=True)
                weights = jnp.exp2((scores - peak) * SCALE2)
                total = jnp.sum(weights, axis=-1, keepdims=True)
                mixed.append(mm(weights.astype(bf16), v_ref[...], NN) * (1.0 / total))
                logs.append(peak * SCALE2 + jnp.log2(total))
            out_ref[rows, :] = jnp.where(left, mixed[0], mixed[1]).astype(bf16)
            turned = jnp.where(left, logs[0], logs[1]).T
            lse_ref[0, :, rows] = jnp.concatenate(
                [turned[0:1], turned[HEAD : HEAD + 1]], axis=0
            )

    return pl.pallas_call(
        kernel,
        name="attend_forward",
        grid_spec=pltpu.PrefetchScalarGridSpec(
            num_scalar_prefetch=1,
            grid=(pairs,),
            in_specs=[
                pl.BlockSpec((length, PAIR), head_columns(width, kind)) for kind in range(3)
            ],
            out_specs=[
                pl.BlockSpec((length, PAIR), pair_columns(width)),
                pl.BlockSpec((1, 2, length), lambda p, ids: (p, 0, 0)),
            ],
        ),
        out_shape=[
            jax.ShapeDtypeStruct((length, width), bf16),
            jax.ShapeDtypeStruct((pairs, 2, length), f32),
        ],
        compiler_params=params(),
        cost_estimate=cost(16 * length * length * width, 8 * length * width),
    )(ids, qkv, qkv, qkv)


def attend_backward(ids, qkv, mixed, grad, lse, block=512):
    length, width3 = qkv.shape
    width = width3 // 3
    pairs = width // PAIR
    per_part = pairs // 4
    cols = 3 * width // 4

    def kernel(
        ids_ref, q_ref, k_ref, v_ref, o_ref, do_ref, lse_ref, out_ref, dk_acc, dv_acc
    ):
        left = lax.broadcasted_iota(jnp.int32, (1, PAIR), 1) < HEAD
        top = lax.broadcasted_iota(jnp.int32, (PAIR, 1), 0) < HEAD
        key = k_ref[...]
        value = v_ref[...]
        blank = jnp.zeros_like(key)
        keys = [jnp.where(left, key, blank), jnp.where(left, blank, key)]
        values = [jnp.where(left, value, blank), jnp.where(left, blank, value)]
        key_turned = key.T
        row = lax.broadcasted_iota(jnp.int32, (8, PAIR), 0)
        lane = lax.broadcasted_iota(jnp.int32, (8, PAIR), 1)
        pick = jnp.where((lane >= HEAD) == (row == 1), 1.0, 0.0).astype(bf16)
        spot = (pl.program_id(0) % per_part) * PAIR

        def window(kind):
            return pl.ds(pl.multiple_of(spot + kind * per_part * PAIR, PAIR), PAIR)

        for b in range(length // block):
            rows = slice(b * block, (b + 1) * block)
            query = q_ref[rows, :]
            out_grad = do_ref[rows, :]
            product = out_grad.astype(f32) * o_ref[rows, :].astype(f32)
            high = product.astype(bf16)
            low = (product - high.astype(f32)).astype(bf16)
            delta = mm(pick, high, NT) + mm(pick, low, NT)
            dq, dk, dv = [], [], []
            for h in range(2):
                scores = mm(keys[h], query, NT)
                weights = jnp.exp2(scores * SCALE2 - lse_ref[0, h : h + 1, rows])
                dv.append(mm(weights.astype(bf16), out_grad, NN))
                grad_weights = mm(values[h], out_grad, NT)
                inner = (weights * (grad_weights - delta[h : h + 1, :])).astype(bf16)
                dk.append(mm(inner, query, NN))
                dq.append(mm(key_turned, inner, NN))
            both = jnp.where(top, dq[0], dq[1]).T
            out_ref[rows, window(0)] = (both * 0.125).astype(bf16)
            dk_sum = jnp.where(left, dk[0], dk[1])
            dv_sum = jnp.where(left, dv[0], dv[1])
            if b == 0:
                dk_acc[...] = dk_sum
                dv_acc[...] = dv_sum
            else:
                dk_acc[...] += dk_sum
                dv_acc[...] += dv_sum
        out_ref[:, window(1)] = (dk_acc[...] * 0.125).astype(bf16)
        out_ref[:, window(2)] = dv_acc[...].astype(bf16)

    return pl.pallas_call(
        kernel,
        name="attend_backward",
        grid_spec=pltpu.PrefetchScalarGridSpec(
            num_scalar_prefetch=1,
            grid=(pairs,),
            in_specs=[
                pl.BlockSpec((length, PAIR), head_columns(width, kind)) for kind in range(3)
            ]
            + [pl.BlockSpec((length, PAIR), pair_columns(width))] * 2
            + [pl.BlockSpec((1, 2, length), lambda p, ids: (p, 0, 0))],
            out_specs=pl.BlockSpec((length, cols), lambda p, ids: (0, p // per_part)),
            scratch_shapes=[pltpu.VMEM((length, PAIR), f32)] * 2,
        ),
        out_shape=jax.ShapeDtypeStruct((length, width3), bf16),
        compiler_params=params(),
        cost_estimate=cost(40 * length * length * width, 16 * length * width),
    )(ids, qkv, qkv, qkv, mixed, grad, lse)


def out_copies(ids_ref, refs, where, weight, sems, width):
    cols = width // 4
    copies = []
    for part in range(4):
        spots, t = where[part]
        source = ([refs[n] for n in spots], t, pl.ds(3 * cols, cols))
        at = pl.multiple_of((ids_ref[0] ^ part) * cols, cols)
        copies += slice_copies(
            ids_ref, source, lambda rows: weight.at[rows, pl.ds(at, cols)], sems, len(copies)
        )
    return copies


def out_forward(ids, image, grad_out, mixed, mod, bias, pieces, tile=256):
    length, width = image.shape
    buffers, where = flat_pieces(pieces)
    count = len(buffers)

    def kernel(ids_ref, image_ref, gy_ref, mixed_ref, mod_ref, bias_ref, *rest):
        refs = rest[:count]
        mid_ref, h2_ref, branch_ref, db2_ref, weight, sems = rest[count:]

        @pl.when(pl.program_id(0) == 0)
        def _():
            copies = out_copies(ids_ref, refs, where, weight, sems, width)
            for copy in copies:
                copy.start()
            for copy in copies:
                copy.wait()

        branch = mm(mixed_ref[...], weight[...], NN) + bias_ref[...]
        mid = image_ref[...].astype(f32) + mod_ref[2:3, :] * branch
        norm, _ = norm_of(mid)
        mid_ref[...] = mid
        h2_ref[...] = (norm * (1.0 + mod_ref[4:5, :]) + mod_ref[3:4, :]).astype(bf16)
        branch_ref[...] = branch.astype(bf16)
        db2_ref[...] = (gy_ref[...].astype(f32) * mod_ref[5:6, :]).astype(bf16)

    slots = 4 * len(where[0][0]) * buffers[0].shape[0]
    row = pl.BlockSpec((tile, width), lambda i: (i, 0))
    return pl.pallas_call(
        kernel,
        name="out_forward",
        grid=(length // tile,),
        in_specs=[smem_spec(), row, row, row, whole_spec(mod.shape), whole_spec(bias.shape)]
        + [any_spec()] * count,
        out_specs=[row] * 4,
        out_shape=[
            jax.ShapeDtypeStruct((length, width), f32),
            jax.ShapeDtypeStruct((length, width), bf16),
            jax.ShapeDtypeStruct((length, width), bf16),
            jax.ShapeDtypeStruct((length, width), bf16),
        ],
        scratch_shapes=[
            pltpu.VMEM((width, width), bf16),
            pltpu.SemaphoreType.DMA((slots,)),
        ],
        compiler_params=params(),
        cost_estimate=cost(2 * length * width * width, 18 * length * width),
    )(ids, image, grad_out, mixed, mod, bias, *buffers)


def feed_forward(ids, h2, db2, bias, up_pieces, down_pieces, parts, carried, shards, tile=256):
    length, width = h2.shape
    hidden = width
    half = hidden // 2
    inner = inner_size(shards)
    outer = shards // inner
    rows = width // shards
    up_buffers, up_where = flat_pieces([up_pieces[p] for p in parts])
    down_buffers, down_where = flat_pieces([down_pieces[p] for p in parts])
    n_up, n_down = len(up_buffers), len(down_buffers)
    steps = len(parts)
    n_carry = len(carried)

    def kernel(ids_ref, h2_ref, db2_ref, bias_ref, *rest):
        up_refs = rest[:n_up]
        down_refs = rest[n_up : n_up + n_down]
        carry_refs = rest[n_up + n_down : n_up + n_down + n_carry]
        branch_ref, dh2_ref, grads_ref, dbias_ref = rest[n_up + n_down + n_carry :][:4]
        up_w, down_w, gel, dpre, up_sems, down_sems, carry_sems = rest[
            n_up + n_down + n_carry + 4 :
        ]
        step = pl.program_id(0)
        part, block = step // 2, step % 2
        size = shards

        def weight_copies(n):
            spots, t = up_where[n]
            up = slice_copies(
                ids_ref,
                ([up_refs[s] for s in spots], t, slice(None)),
                lambda r: up_w.at[n, r, :],
                up_sems,
                n * size,
            )
            spots, t = down_where[n]
            down = slice_copies(
                ids_ref,
                ([down_refs[s] for s in spots], t, slice(None)),
                lambda r: down_w.at[n, r, :],
                down_sems,
                n * size,
            )
            return up, down

        def carry_copies():
            return [
                pltpu.make_async_copy(source, target, carry_sems.at[n])
                for n, (source, target) in enumerate(zip(carry_refs, (branch_ref, dh2_ref)))
            ]

        @pl.when(step == 0)
        def _():
            for n in range(steps):
                up, down = weight_copies(n)
                for copy in up + down:
                    copy.start()
            for copy in carry_copies():
                copy.start()
            if not n_carry:
                branch_ref[...] = jnp.zeros_like(branch_ref)
                dh2_ref[...] = jnp.zeros_like(dh2_ref)

        for n in range(steps):

            @pl.when(step == 2 * n)
            def _():
                up, down = weight_copies(n)
                for copy in up + down:
                    copy.wait()

        if n_carry:

            @pl.when(step == 0)
            def _():
                for copy in carry_copies():
                    copy.wait()

        columns = pl.ds(pl.multiple_of(block * half, half), half)
        which = parts[0]
        for n in range(1, steps):
            which = jnp.where(part == n, parts[n], which)
        row = bias_ref[pl.ds(ids_ref[0] ^ which, 1), columns]
        up = up_w[part, :, columns]
        down = down_w[part, columns, :]
        bias_sum = jnp.zeros((1, half), f32)
        for b in range(length // tile):
            tokens = slice(b * tile, (b + 1) * tile)
            grad = db2_ref[tokens, :]
            pre = mm(h2_ref[tokens, :], up, NN) + row
            square = pre * pre
            bend = jnp.tanh(GELU_C * pre * (1.0 + 0.044715 * square))
            lift = 0.5 * (1.0 + bend)
            slope = lift + 0.5 * pre * (1.0 - bend * bend) * (
                GELU_C * (1.0 + 3.0 * 0.044715 * square)
            )
            active = (pre * lift).astype(bf16)
            change = (mm(grad, down, NT) * slope).astype(bf16)
            gel[tokens, :] = active
            dpre[tokens, :] = change
            bias_sum += jnp.sum(change.astype(f32), axis=0, keepdims=True)
            branch_ref[tokens, :] += mm(active, down, NN)
            dh2_ref[tokens, :] += mm(change, up, NT)
        dbias_ref[0, :, columns] = bias_sum

        def slot(s):
            offset = ids_ref[1] ^ s
            return offset % inner, offset // inner

        grad_up = mm(h2_ref[...], dpre[...], TN)
        for s in range(shards):
            j, k = slot(s)
            grads_ref[0, j, k, 0, :, columns] = grad_up[s * rows : (s + 1) * rows, :].astype(bf16)
        grad_down = mm(gel[...], db2_ref[...], TN)
        for s in range(shards // 2):
            j, k = slot(block * (shards // 2) + s)
            grads_ref[0, j, k, 1, :, :] = grad_down[s * rows : (s + 1) * rows, :].astype(bf16)

    single = pl.Buffered(1)
    acts = pl.BlockSpec((length, width), lambda i: (0, 0), pipeline_mode=single)
    sums = pl.BlockSpec((length, width), lambda i: (0, 0), pipeline_mode=single)
    return pl.pallas_call(
        kernel,
        name="feed_forward",
        grid=(2 * steps,),
        in_specs=[smem_spec(), acts, acts, whole_spec(bias.shape)]
        + [any_spec()] * (n_up + n_down + n_carry),
        out_specs=[
            sums,
            sums,
            pl.BlockSpec(
                (1, inner, outer, 2, rows, width), lambda i: (i // 2, 0, 0, 0, 0, 0)
            ),
            pl.BlockSpec((1, 1, hidden), lambda i: (i // 2, 0, 0)),
        ],
        out_shape=[
            jax.ShapeDtypeStruct((length, width), f32),
            jax.ShapeDtypeStruct((length, width), f32),
            jax.ShapeDtypeStruct((steps, inner, outer, 2, rows, width), bf16),
            jax.ShapeDtypeStruct((steps, 1, hidden), f32),
        ],
        scratch_shapes=[
            pltpu.VMEM((steps, width, hidden), bf16),
            pltpu.VMEM((steps, hidden, width), bf16),
            pltpu.VMEM((length, half), bf16),
            pltpu.VMEM((length, half), bf16),
            pltpu.SemaphoreType.DMA((steps * shards,)),
            pltpu.SemaphoreType.DMA((steps * shards,)),
            pltpu.SemaphoreType.DMA((2,)),
        ],
        compiler_params=params(),
        cost_estimate=cost(12 * steps * length * width * hidden, 40 * length * width),
    )(ids, h2, db2, bias, *up_buffers, *down_buffers, *carried)


def middle_backward(
    ids, mid, branch2, dh2, grad_out, branch1, mod, down_bias, pieces, tile=256
):
    length, width = mid.shape
    buffers, where = flat_pieces(pieces)
    count = len(buffers)

    def kernel(
        ids_ref, mid_ref, branch2_ref, dh2_ref, gy_ref, branch1_ref, mod_ref, bias_ref, *rest
    ):
        refs = rest[:count]
        out_ref, dmid_ref, db1_ref, datt_ref, sums_ref, weight, sems = rest[count:]

        @pl.when(pl.program_id(0) == 0)
        def _():
            copies = out_copies(ids_ref, refs, where, weight, sems, width)
            for copy in copies:
                copy.start()
            sums_ref[...] = jnp.zeros_like(sums_ref)
            for copy in copies:
                copy.wait()

        def total(row, values):
            sums_ref[row : row + 1, :] += jnp.sum(values, axis=0, keepdims=True)

        mid = mid_ref[...]
        grad = gy_ref[...].astype(f32)
        gate1, gate2 = mod_ref[2:3, :], mod_ref[5:6, :]
        branch = branch2_ref[...] + bias_ref[...]
        out_ref[...] = (mid + gate2 * branch).astype(bf16)
        total(0, grad * branch)
        total(1, (grad * gate2).astype(bf16).astype(f32))
        norm, inverse = norm_of(mid)
        dh2 = dh2_ref[...]
        total(2, dh2)
        total(3, dh2 * norm)
        dmid = grad + norm_back(norm, inverse, dh2 * (1.0 + mod_ref[4:5, :]))
        dmid_ref[...] = dmid
        total(4, dmid * branch1_ref[...].astype(f32))
        db1 = (dmid * gate1).astype(bf16)
        db1_ref[...] = db1
        total(5, db1.astype(f32))
        datt_ref[...] = mm(db1, weight[...], NT).astype(bf16)

    slots = 4 * len(where[0][0]) * buffers[0].shape[0]
    row = pl.BlockSpec((tile, width), lambda i: (i, 0))
    return pl.pallas_call(
        kernel,
        name="middle_backward",
        grid=(length // tile,),
        in_specs=[smem_spec()] + [row] * 5 + [whole_spec(mod.shape), whole_spec(down_bias.shape)]
        + [any_spec()] * count,
        out_specs=[row] * 4 + [whole_spec((8, width))],
        out_shape=[
            jax.ShapeDtypeStruct((length, width), bf16),
            jax.ShapeDtypeStruct((length, width), f32),
            jax.ShapeDtypeStruct((length, width), bf16),
            jax.ShapeDtypeStruct((length, width), bf16),
            jax.ShapeDtypeStruct((8, width), f32),
        ],
        scratch_shapes=[
            pltpu.VMEM((width, width), bf16),
            pltpu.SemaphoreType.DMA((slots,)),
        ],
        compiler_params=params(),
        cost_estimate=cost(2 * length * width * width, 30 * length * width),
    )(ids, mid, branch2, dh2, grad_out, branch1, mod, down_bias, *buffers)


def attention_grads(ids, h1, grad_qkv, mixed, grad_branch, parts, shards):
    length, width = h1.shape
    cols = 3 * width // 4
    rest_cols = width - cols
    inner = inner_size(shards)
    outer = shards // inner
    rows = width // shards

    def part_of(i):
        which = parts[0]
        for n in range(1, len(parts)):
            which = jnp.where(i == n, parts[n], which)
        return which

    def kernel(ids_ref, h1_ref, dqkv_ref, mixed_ref, db1_ref, out_ref):
        first = mm(h1_ref[...], dqkv_ref[...], TN)
        second = mm(mixed_ref[...], db1_ref[...], TN)
        for s in range(shards):
            offset = ids_ref[1] ^ s
            j, k = offset % inner, offset // inner
            window = slice(s * rows, (s + 1) * rows)
            out_ref[0, j, k, :, :cols] = first[window, :].astype(bf16)
            out_ref[0, j, k, :, cols:] = second[window, :].astype(bf16)

    acts = pl.BlockSpec((length, width), lambda i, ids: (0, 0), pipeline_mode=pl.Buffered(1))
    return pl.pallas_call(
        kernel,
        name="attention_grads",
        grid_spec=pltpu.PrefetchScalarGridSpec(
            num_scalar_prefetch=1,
            grid=(len(parts),),
            in_specs=[
                acts,
                pl.BlockSpec((length, cols), lambda i, ids: (0, part_of(i))),
                acts,
                pl.BlockSpec((length, rest_cols), lambda i, ids: (0, ids[0] ^ part_of(i))),
            ],
            out_specs=pl.BlockSpec(
                (1, inner, outer, rows, width), lambda i, ids: (i, 0, 0, 0, 0)
            ),
        ),
        out_shape=jax.ShapeDtypeStruct((len(parts), inner, outer, rows, width), bf16),
        compiler_params=params(),
        cost_estimate=cost(2 * len(parts) * length * width * width, 12 * length * width),
    )(ids, h1, grad_qkv, mixed, grad_branch)


def image_backward(ids, image, grad_mid, grad_qkv, mod, pieces, tile=256):
    length, width = image.shape
    cols = 3 * width // 4
    buffers, where = flat_pieces(pieces)
    count = len(buffers)

    def kernel(ids_ref, image_ref, dmid_ref, dqkv_ref, mod_ref, *rest):
        refs = rest[:count]
        out_ref, sums_ref, bias_ref, weight, sems = rest[count:]
        first = pl.program_id(0) == 0

        def copies(part):
            spots, t = where[part]
            source = ([refs[n] for n in spots], t, pl.ds(0, cols))
            size = len(spots) * refs[0].shape[0]
            return slice_copies(
                ids_ref, source, lambda rows: weight.at[part, rows, :], sems, part * size
            )

        @pl.when(first)
        def _():
            for part in range(4):
                for copy in copies(part):
                    copy.start()
            sums_ref[...] = jnp.zeros_like(sums_ref)
            bias_ref[...] = jnp.zeros_like(bias_ref)
            for part in range(4):
                for copy in copies(part):
                    copy.wait()

        dqkv = dqkv_ref[...]
        bias_ref[...] += jnp.sum(dqkv.astype(f32), axis=0, keepdims=True)
        grad = mm(dqkv[:, :cols], weight[0], NT)
        for part in range(1, 4):
            grad += mm(dqkv[:, part * cols : (part + 1) * cols], weight[part], NT)
        norm, inverse = norm_of(image_ref[...].astype(f32))
        sums_ref[0:1, :] += jnp.sum(grad, axis=0, keepdims=True)
        sums_ref[1:2, :] += jnp.sum(grad * norm, axis=0, keepdims=True)
        out_ref[...] = dmid_ref[...] + norm_back(norm, inverse, grad * (1.0 + mod_ref[1:2, :]))

    slots = 4 * len(where[0][0]) * buffers[0].shape[0]
    row = pl.BlockSpec((tile, width), lambda i: (i, 0))
    return pl.pallas_call(
        kernel,
        name="image_backward",
        grid=(length // tile,),
        in_specs=[
            smem_spec(),
            row,
            row,
            pl.BlockSpec((tile, 3 * width), lambda i: (i, 0)),
            whole_spec(mod.shape),
        ]
        + [any_spec()] * count,
        out_specs=[row, whole_spec((8, width)), whole_spec((1, 3 * width))],
        out_shape=[
            jax.ShapeDtypeStruct((length, width), f32),
            jax.ShapeDtypeStruct((8, width), f32),
            jax.ShapeDtypeStruct((1, 3 * width), f32),
        ],
        scratch_shapes=[
            pltpu.VMEM((4, width, cols), bf16),
            pltpu.SemaphoreType.DMA((slots,)),
        ],
        compiler_params=params(),
        cost_estimate=cost(6 * length * width * width, 18 * length * width),
    )(ids, image, grad_mid, grad_qkv, mod, *buffers)


def own_features(timestep, start, count, total_width):
    half = total_width // 2
    column = start + jnp.arange(count)
    place = (column % half).astype(f32)
    frequency = jnp.exp(-math.log(10000.0) * place / half)
    angles = timestep[:, None] * frequency[None, :]
    return jnp.where(column[None, :] < half, jnp.cos(angles), jnp.sin(angles))


def shards_program(
    image,
    timestep,
    label,
    label_table,
    ada_weight,
    ada_bias,
    qkv_weight,
    qv_bias,
    out_weight,
    out_bias,
    up_weight,
    up_bias,
    down_weight,
    down_bias,
    grad_out,
):
    shards = lax.axis_size("shard")
    me = lax.axis_index("shard")
    rep = lax.axis_index("rep")
    ids = jnp.stack([rep, me]).astype(jnp.int32)
    _, length, width = image.shape
    image2 = image[0]
    gy = grad_out[0]
    slice_rows = width // shards
    wide = 4 * width
    unit = wide // shards // 4
    shard_bits = bits_of(shards)

    own_bias = jnp.concatenate([qv_bias, out_bias, up_bias, down_bias]).astype(f32)
    n_bias = own_bias.shape[0]
    meta = jnp.concatenate(
        [label.astype(f32), timestep.astype(f32), jnp.zeros((126,), f32)]
    )
    front = jnp.concatenate([own_bias, meta]).reshape(1, -1, 128)
    front = gather_xor(front, "shard", shard_bits)
    bias_all = unxor(front[:, :-1].reshape(shards, n_bias), me, shards)
    meta_rep = front[:, -1]

    def condition_of(entries):
        names = lax.broadcasted_iota(jnp.int32, (entries.shape[0], label_table.shape[0]), 1)
        hot = entries[:, 0:1].astype(jnp.int32) == names
        rows = jnp.dot(hot.astype(bf16), label_table, preferred_element_type=f32)
        return hot, rows + own_features(entries[:, 1], me * slice_rows, slice_rows, width)

    _, cond_rep = condition_of(meta_rep)
    act_rep = jax.nn.silu(cond_rep).astype(bf16)
    mod = jnp.dot(act_rep, ada_weight, preferred_element_type=f32)
    bias_row = lax.dynamic_update_slice_in_dim(
        jnp.zeros((6 * width,), f32), ada_bias.astype(f32), me * ada_bias.shape[0], 0
    )
    mod = mod + bias_row[None, :]
    for bit in reversed(shard_bits):
        mod = mod[:bit] + swap(mod[bit:], "shard", bit)
    mod = mod.reshape(6, width)

    attn_parts = jnp.concatenate(
        [qkv_weight.reshape(slice_rows, 3, 4, width // 4), out_weight.reshape(slice_rows, 1, 4, width // 4)],
        axis=1,
    )
    attn_parts = attn_parts.transpose(2, 0, 1, 3).reshape(4, slice_rows, width)
    up_parts = (
        up_weight.reshape(slice_rows, shards, 4, unit)
        .transpose(2, 0, 1, 3)
        .reshape(4, slice_rows, width)
    )
    down_parts = down_weight.reshape(4, unit, width)
    attn_w = gather_full(attn_parts, rep, shards)
    up_parts, _ = lax.optimization_barrier((up_parts, attn_w[0][0][0]))
    up_w = gather_full(up_parts, rep, shards)
    down_parts, _ = lax.optimization_barrier((down_parts, up_w[0][0][0]))
    down_w = gather_half(down_parts, rep, shards)

    def cut(start, count):
        return bias_all[:, start : start + count].reshape(1, -1)

    at = 0
    fulls = []
    for piece in (qv_bias, out_bias, up_bias, down_bias):
        fulls.append(cut(at, piece.shape[0]))
        at += piece.shape[0]
    qv_full, out_full, up_full, down_full = fulls
    qv_full = qv_full.reshape(2, 4, width // 4)
    qkv_bias = jnp.stack([qv_full[0], jnp.zeros_like(qv_full[0]), qv_full[1]], axis=1)
    qkv_bias = qkv_bias.reshape(4, 3 * width // 4)
    up_full = up_full.reshape(shards, 4, unit).transpose(1, 0, 2).reshape(4, width)

    h1, qkv = qkv_forward(ids, image2, mod, qkv_bias, attn_w)
    mixed, lse = attend_forward(ids, qkv)
    mid, h2, branch1, db2 = out_forward(ids, image2, gy, mixed, mod, out_full, attn_w)
    branch2, dh2, ff_send, dup_send = feed_forward(
        ids, h2, db2, up_full, up_w, down_w, (3, 1), (), shards
    )
    branch2, dh2, ff_keep, dup_keep = feed_forward(
        ids, h2, db2, up_full, up_w, down_w, (2, 0), (branch2, dh2), shards
    )
    ff_own = scatter_sum(ff_keep, ff_send, shards)
    ff_all = gather_quarters(ff_own, rep)

    output, dmid, db1, datt, sums2 = middle_backward(
        ids, mid, branch2, dh2, gy, branch1, mod, down_full, attn_w
    )
    dqkv = attend_backward(ids, qkv, mixed, datt, lse)
    at_send = attention_grads(ids, h1, dqkv, mixed, db1, (3, 1), shards)
    at_keep = attention_grads(ids, h1, dqkv, mixed, db1, (2, 0), shards)
    at_own = scatter_sum(at_keep, at_send, shards)
    at_all = gather_quarters(at_own, rep)
    grad_image, sums1, qkv_sums = image_backward(ids, image2, dmid, dqkv, mod, attn_w)

    qkv_sums = unxor(qkv_sums.reshape(4, 3, width // 4), rep, 4)
    dup = jnp.concatenate([dup_keep[1:], dup_send[1:], dup_keep[:1], dup_send[:1]], axis=0)
    dup = unxor(dup.reshape(4, width), rep, 4).reshape(4, shards, unit).transpose(1, 0, 2)
    tail = jnp.concatenate(
        [
            sums1[0],
            sums1[1],
            sums2[4],
            sums2[2],
            sums2[3],
            sums2[0],
            qkv_sums[:, 0].reshape(-1),
            qkv_sums[:, 2].reshape(-1),
            sums2[5],
            dup.reshape(-1),
            sums2[1],
        ]
    ).astype(bf16)
    tail = tail.reshape(1, 14, width)
    tail = gather_xor(tail, "shard", shard_bits[::-1])
    tail = gather_xor(tail, "rep", [2, 1])
    images = tail.shape[0]
    dmod_all = tail[:, :6].reshape(images, 6 * width)
    bias_grads = jnp.sum(tail[:, 6:].astype(f32), axis=0).reshape(-1)

    metas = gather_xor(meta_rep[None], "rep", [1, 2])
    levels = len(shard_bits)
    metas = metas.reshape(2, 2, *([2] * levels), 128)
    metas = metas.transpose(1, 0, *range(1 + levels, 1, -1), 2 + levels).reshape(images, 128)
    hot, cond = condition_of(metas)
    act, silu_back = jax.vjp(jax.nn.silu, cond)
    ada_part = lax.dot_general(act.astype(bf16), dmod_all, TN, preferred_element_type=f32)
    own_cols = 6 * width // shards
    ada_bias_part = jnp.sum(
        lax.dynamic_slice_in_dim(dmod_all, me * own_cols, own_cols, 1), axis=0, dtype=f32
    )
    grad_act = lax.dot_general(dmod_all, ada_weight, NT, preferred_element_type=f32)
    (grad_cond_all,) = silu_back(grad_act)
    table_part = jnp.dot(
        hot.astype(f32).T,
        grad_cond_all,
        precision=lax.Precision.HIGHEST,
        preferred_element_type=f32,
    )
    mine = grad_cond_all[:shards].reshape(*([2] * levels), slice_rows)
    mine = mine.transpose(*range(levels - 1, -1, -1), levels).reshape(1, shards, slice_rows)
    every = gather_xor(mine, "shard", shard_bits)
    diagonal = jnp.stack([every[m, m] for m in range(shards)])
    grad_cond = unxor(diagonal, me, shards).reshape(1, width)

    ff_all = ff_all.astype(f32)
    grad_up = (
        ff_all[:, 0]
        .reshape(4, slice_rows, shards, unit)
        .transpose(1, 2, 0, 3)
        .reshape(slice_rows, wide)
    )
    grad_down = ff_all[:, 1].reshape(4 * unit, width)
    at_all = at_all.astype(f32).reshape(4, slice_rows, 4, width // 4)
    grad_qkv = at_all[:, :, :3].transpose(1, 2, 0, 3).reshape(slice_rows, 3 * width)
    grad_out_w = at_all[:, :, 3].transpose(1, 0, 2).reshape(slice_rows, width)

    def own(start, count):
        piece = bias_grads[start : start + count]
        return lax.dynamic_slice_in_dim(piece, me * (count // shards), count // shards, 0)

    return (
        output[None],
        grad_image[None],
        grad_cond,
        table_part,
        ada_part,
        ada_bias_part,
        grad_qkv,
        own(0, 2 * width),
        grad_out_w,
        own(2 * width, width),
        grad_up,
        own(3 * width, wide),
        grad_down,
        own(3 * width + wide, width),
    )


def solution(mesh):
    both = ("rep", "shard")
    return jax.shard_map(
        shards_program,
        mesh=mesh,
        in_specs=(
            P(both, None, None),
            P(both),
            P(both),
            P(None, "shard"),
            P("shard", None),
            P("shard"),
            P("shard", None),
            P("shard"),
            P("shard", None),
            P("shard"),
            P("shard", None),
            P("shard"),
            P("shard", None),
            P("shard"),
            P(both, None, None),
        ),
        out_specs=(
            P(both, None, None),
            P(both, None, None),
            P(both, None),
            P(None, "shard"),
            P("shard", None),
            P("shard"),
            P("shard", None),
            P("shard"),
            P("shard", None),
            P("shard"),
            P("shard", None),
            P("shard"),
            P("shard", None),
            P("shard"),
        ),
        check_vma=False,
    )
```
